256 devices in a mesh: wide: 64 (over y, x, z_lo), narrow: 4 (over z_hi, core).
Axes of the slice: x: 4, y: 4, z: 8 (z_hi: 2, z_lo: 4; z = z_hi * 4 + z_lo), core: 2. Of those that a mesh axis runs over, the one named last changes fastest.
Arguments:
- volume: float32 [1024, 48, 1024], P('wide', None, 'narrow'), may hold values from 0 to 2
- codes_in: bfloat16 [1024, 72, 1536], P('wide', None, 'narrow'), may hold values from -4 to 4
- x_transform: float32 [1024, 1024], replicated, may hold values from -1 to 1, as said below
- y_atoms: bfloat16 [1024, 1536], replicated, may hold values from -0.1875 to 0.1875
- de_atoms: bfloat16 [48, 72], replicated, may hold values from -0.875 to 0.875
Outputs:
- codes_out: bfloat16 [1024, 72, 1536], P('wide', None, 'narrow')
- estimate: bfloat16 [1024, 48, 1024], P('wide', None, 'narrow')
The draws below stay inside these ranges and needn't reach their ends.
Inputs may be any that keep to these rules, and one draw needn't show every extreme that they name: x_transform is orthonormal: its transpose is its inverse.
All inputs are finite; a program needn't handle non-finite values.
Results may differ from the reference program's by a relative error of at most 0.0065.
Values may be sent and summed in bfloat16 or wider, within the bound.
A program may use at most 64 MiB of HBM per device.

```python
import jax
import jax.numpy as jnp
from jax import lax

NX = 1024
NY = 1024
NE = 48
KY = 1536
KE = 72
ITERS = 1


def draw_x_transform(key, part):
    normal_table = jax.random.normal(jax.random.fold_in(key, 7), (NX, NX), jnp.float32)
    factor_q, factor_r = jnp.linalg.qr(normal_table)
    return factor_q * jnp.sign(jnp.diagonal(factor_r))[None, :]


def shard_levels(key, extent, pieces, low, largest):
    factor_of, own = 1.0, jax.random.fold_in(key, 6)
    for dim, blocks in pieces:
        steps = jnp.exp(jax.random.uniform(jax.random.fold_in(own, dim), (blocks,), jnp.float32, low / len(pieces), largest / len(pieces)))
        factor_of = factor_of * jnp.repeat(steps, extent[dim] // blocks).reshape([-1 if axis == dim else 1 for axis in range(len(extent))])
    return factor_of


def noise(rng, dims, deviation, most, pieces=(), held_as=jnp.bfloat16):
    array = jax.random.normal(rng, dims, jnp.float32) * deviation
    if len(pieces) > 0:
        array = shard_levels(rng, dims, pieces, -0.22, 0.18) * array
    return jnp.clip(array, min=-most, max=most).astype(held_as)


def setup_inputs(seed: int = 0) -> dict:
    streams_of = jax.random.split(jax.random.key(seed), 6)
    volume = jnp.clip(2.0 * jax.random.uniform(streams_of[0], (NX, NE, NY), jnp.float32) ** shard_levels(streams_of[0], (NX, NE, NY), ((0, 64), (2, 4)), -0.2, 0.2), 0.0, 2.0)
    codes_in = noise(streams_of[1], (NX, KE, KY), 0.5, 4.0, ((0, 64), (2, 4)))
    x_transform = draw_x_transform(jax.random.fold_in(streams_of[5], 71), 0)
    y_atoms = noise(streams_of[3], (NY, KY), NY ** -0.5, 0.1875)
    de_atoms = noise(streams_of[4], (NE, KE), NE ** -0.5, 0.875)
    return {"volume": volume, "codes_in": codes_in, "x_transform": x_transform, "y_atoms": y_atoms, "de_atoms": de_atoms}


step_size = 0.06
threshold = 0.05
block_rows = 16
best = lax.Precision.HIGHEST

def rebuild(codes, de32, dy32):
    atoms = jnp.einsum('fk,bkc->bfc', de32, codes.astype(jnp.float32), precision=best).astype(jnp.bfloat16)
    return jnp.einsum('bfc,yc->bfy', atoms.astype(jnp.float32), dy32, precision=best)

def solve_block(pair, de32, dy32):
    target, codes = pair
    for step in range(ITERS):
        misfit = rebuild(codes, de32, dy32) - target
        pulled = jnp.einsum('fk,bfy->bky', de32, misfit, precision=best).astype(jnp.bfloat16)
        grads = jnp.einsum('bky,yc->bkc', pulled.astype(jnp.float32), dy32, precision=best)
        moved = codes.astype(jnp.float32) - step_size * grads
        codes = (moved - jnp.clip(moved, -threshold, threshold)).astype(jnp.bfloat16)
    return (codes, rebuild(codes, de32, dy32))

def reference(volume, codes_in, x_transform, y_atoms, de_atoms):
    flat = volume.reshape(NX, NE * NY)
    target = jnp.dot(x_transform, flat, precision=best).reshape(NX // block_rows, block_rows, NE, NY)
    blocks = codes_in.reshape(NX // block_rows, block_rows, KE, KY)
    de32 = de_atoms.astype(jnp.float32)
    dy32 = y_atoms.astype(jnp.float32)
    codes_out, image = lax.map(lambda pair: solve_block(pair, de32, dy32), (target, blocks))
    codes_out = codes_out.reshape(NX, KE, KY)
    image = image.reshape(NX, NE * NY)
    back = lax.dot_general(x_transform, image, (((0,), (0,)), ((), ())), precision=best)
    estimate = jnp.maximum(back, 0.0).astype(jnp.bfloat16).reshape(NX, NE, NY)
    return (codes_out, estimate)
```

```python
import jax
import jax.numpy as jnp
from jax import lax
from jax.experimental import pallas as pl
from jax.experimental.pallas import tpu as pltpu
from jax.sharding import PartitionSpec as P

step_size = 0.06
threshold = 0.05
BF = jnp.bfloat16
F32 = jnp.float32
MESH = pl.DeviceIdType.MESH


def mm(a, b):
    return jnp.dot(a, b, preferred_element_type=F32)


def nt(a, b):
    return lax.dot_general(a, b, (((1,), (1,)), ((), ())), preferred_element_type=F32)


def tn(a, b):
    return lax.dot_general(a, b, (((0,), (0,)), ((), ())), preferred_element_type=F32)


def shrink(codes, grads):
    moved = codes - step_size * grads
    return (moved - jnp.clip(moved, -threshold, threshold)).astype(BF)


def remote(src, dst, send, recv, device):
    return pltpu.make_async_remote_copy(
        src_ref=src, dst_ref=dst, send_sem=send, recv_sem=recv, device_id=device, device_id_type=MESH
    )


def kernel(
    vol, codes, xin, din, de,
    new_codes, est,
    xv, xrows, xcols, dv, codes4, send1, recv1, send2, recv2, send3, recv3, send4, recv4, qsend, qrecv, atoms, fresh,
    xsem, dsem, ssem1, rsem1, fsem1, gsem1, ssem2, rsem2, ssem3, rsem3, fsem3, gsem3, ssem4, rsem4,
    csend, crecv, qssem, qrsem, lsem,
):
    w = lax.axis_index("wide")
    n = lax.axis_index("narrow")
    half = n // 2
    core = n % 2
    chip = 2 * w + half
    twin = (w, 2 * half + 1 - core)
    bit = lax.rem(w // 2, 2)

    load_x = pltpu.make_async_copy(xin, xv, xsem)
    load_d = pltpu.make_async_copy(din, dv, dsem)
    load_x.start()
    load_d.start()

    barrier = pltpu.get_barrier_semaphore()

    def greet_to(i, c):
        to = 4 * (i // 2) + 2 * core + lax.rem(i, 2)
        pl.semaphore_signal(barrier, inc=1, device_id=(to, 2 * half + 1 - bit), device_id_type=MESH)
        return c

    def greet_from(i, c):
        frm = 4 * (i // 2) + 2 * (1 - core) + lax.rem(i, 2)
        pl.semaphore_signal(barrier, inc=1, device_id=(frm, 2 * half + bit), device_id_type=MESH)
        return c

    for d in (1, 2, 3):
        pl.semaphore_signal(barrier, inc=1, device_id=(w, lax.rem(n + d, 4)), device_id_type=MESH)
    lax.fori_loop(0, 32, greet_to, 0)
    lax.fori_loop(0, 32, greet_from, 0)

    for f in range(48):
        rows = vol[:, f, :].astype(BF)
        for b in range(2):
            send1[f // 3, b, f % 3] = rows[:, 128 * b : 128 * b + 128]

    pl.semaphore_wait(barrier, 67)

    def start1(i, c):
        t = lax.rem(w // 4 + i // 2, 16)
        b = lax.rem(w + i, 2)
        remote(
            send1.at[t, b], recv1.at[w // 4, bit, lax.rem(w, 2)], ssem1, rsem1, (4 * t + 2 * core + b, 2 * half + 1 - bit)
        ).start()
        return c

    lax.fori_loop(0, 32, start1, 0)
    for d in (2, 3, 1):
        other = lax.rem(n + d, 4)
        remote(codes.at[pl.ds(4 * other, 4)], codes4.at[n], csend, crecv, (w, other)).start()
    own_codes = pltpu.make_async_copy(codes.at[pl.ds(4 * n, 4)], codes4.at[n], lsem.at[0])
    own_codes.start()

    load_x.wait()

    def group_rows(i, c):
        rows = xv[pl.ds(pl.multiple_of(64 * i, 64), 64), :].reshape(8, 8, 1024)
        for s in range(2):
            xrows[s, pl.ds(pl.multiple_of(32 * i, 32), 32), :] = rows[:, 4 * s : 4 * s + 4].reshape(32, 1024).astype(BF)
        return c

    lax.fori_loop(0, 16, group_rows, 0)

    pltpu.make_async_copy(send1, recv1.at[:, 1 - core], rsem1).wait()
    forward = remote(recv1.at[:, 1 - core], recv1.at[:, 1 - core], fsem1, gsem1, twin)
    forward.start()
    pltpu.make_async_copy(send1, recv1.at[:, core], gsem1).wait()
    for f in range(3):
        mixed = mm(xrows[core], recv1[:, :, :, f].reshape(1024, 128))
        send2[:, f] = mixed.reshape(128, 4, 128).astype(BF)

    def start2(i, c):
        to = lax.rem(chip + 1 + i, 128)
        remote(send2.at[to], recv2.at[chip], ssem2, rsem2, (to // 2, 2 * lax.rem(to, 2) + core)).start()
        return c

    lax.fori_loop(0, 127, start2, 0)
    own2 = pltpu.make_async_copy(send2.at[chip], recv2.at[chip], lsem.at[1])
    own2.start()

    for s in range(2):

        def flip(i, c):
            part = xrows[s, :, pl.ds(pl.multiple_of(128 * i, 128), 128)].astype(F32)
            xcols[s, pl.ds(2 * i, 2)] = part.T.reshape(2, 2, 32, 512).astype(BF)
            return c

        lax.fori_loop(0, 8, flip, 0)

    load_d.wait()
    pltpu.make_async_copy(codes4.at[0:3], codes4.at[0:3], crecv).wait()
    own_codes.wait()
    for m in range(4):
        atoms[:, 384 * m : 384 * m + 384] = mm(de[...], codes4[m].reshape(288, 384)).astype(BF)
    image = nt(atoms[...], dv[...])

    pltpu.make_async_copy(send2.at[0:127], recv2.at[0:127], rsem2).wait()
    own2.wait()
    got = recv2[...].reshape(16, 4, 2, 3, 4, 128)
    target = jnp.concatenate(
        [got[:, b, h].reshape(192, 128) for h in range(2) for b in range(4)], axis=1
    )
    misfit = (image - target.astype(F32)).astype(BF)
    for m in range(4):
        q = mm(misfit, dv[:, 384 * m : 384 * m + 384]).astype(BF)
        qsend[m] = q
        old = codes4[m].reshape(288, 384).astype(F32)
        fresh[m] = shrink(old, tn(de[...], q))
    for d in (2, 3, 1):
        other = lax.rem(n + d, 4)
        remote(qsend.at[other], qrecv.at[n], qssem, qrsem, (w, other)).start()
    own_q = pltpu.make_async_copy(qsend.at[n], qrecv.at[n], lsem.at[2])
    own_q.start()
    for m in range(4):
        atoms[:, 384 * m : 384 * m + 384] = mm(de[...], fresh[m]).astype(BF)
    for h in range(2):
        for b in range(4):
            block = nt(atoms[...], dv[512 * h + 128 * b : 512 * h + 128 * b + 128, :])
            send3[:, 2 * b + h] = block.reshape(16, 3, 4, 128).astype(BF)

    def start3(i, c):
        to = lax.rem(chip + 1 + i, 128)
        remote(
            send3.at[to // 8, lax.rem(to, 8)], recv3.at[core, chip], ssem3, rsem3, (to // 2, 2 * lax.rem(to, 2) + core)
        ).start()
        return c

    lax.fori_loop(0, 127, start3, 0)
    own3 = pltpu.make_async_copy(send3.at[chip // 8, lax.rem(chip, 8)], recv3.at[core, chip], lsem.at[3])
    own3.start()
    pltpu.make_async_copy(send2.at[0:127], recv3.at[core, 0:127], rsem3).wait()
    own3.wait()
    forward3 = remote(recv3.at[core], recv3.at[core], fsem3, gsem3, twin)
    forward3.start()
    pltpu.make_async_copy(send2, recv3.at[1 - core], gsem3).wait()

    for f in range(3):
        back = mm(xcols[0, :, 1 - core].reshape(512, 512), recv3[0, :, f].reshape(512, 128))
        back += mm(xcols[1, :, 1 - core].reshape(512, 512), recv3[1, :, f].reshape(512, 128))
        send4[:, :, f] = jnp.maximum(back, 0.0).reshape(16, 2, 16, 128).astype(BF)

    def start4(i, c):
        a = lax.rem(w // 4 + i // 2, 16)
        b = lax.rem(w + i, 2)
        to = 4 * a + 2 * (1 - core) + b
        remote(send4.at[a, b], recv4.at[w // 4, lax.rem(w, 2)], ssem4, rsem4, (to, 2 * half + bit)).start()
        return c

    lax.fori_loop(0, 32, start4, 0)

    pltpu.make_async_copy(qsend.at[0:3], qrecv.at[0:3], qrsem).wait()
    own_q.wait()
    for m in range(4):
        old = codes[4 * m : 4 * m + 4].reshape(288, 384).astype(F32)
        new_codes[4 * m : 4 * m + 4] = shrink(old, tn(de[...], qrecv[m])).reshape(4, 72, 384)

    pltpu.make_async_copy(send4, recv4, rsem4).wait()
    est[...] = recv4[...]

    pltpu.make_async_copy(send1, send1, ssem1).wait()
    pltpu.make_async_copy(send1, send1, fsem1).wait()
    pltpu.make_async_copy(send2.at[0:127], send2.at[0:127], ssem2).wait()
    pltpu.make_async_copy(send2.at[0:127], send2.at[0:127], ssem3).wait()
    pltpu.make_async_copy(send2, send2, fsem3).wait()
    pltpu.make_async_copy(send4, send4, ssem4).wait()
    pltpu.make_async_copy(codes4.at[0:3], codes4.at[0:3], csend).wait()
    pltpu.make_async_copy(qsend.at[0:3], qsend.at[0:3], qssem).wait()


def shards(volume, codes_in, x_transform, y_atoms, de_atoms):
    eye = jnp.eye(4, dtype=BF)
    de = (de_atoms[:, None, None, :] * eye[None, :, :, None]).reshape(192, 288)
    dma = pltpu.SemaphoreType.DMA
    vmem = pl.BlockSpec(memory_space=pltpu.VMEM)
    anyspace = pl.BlockSpec(memory_space=pl.ANY)
    codes_out, est = pl.pallas_call(
        kernel,
        out_shape=(
            jax.ShapeDtypeStruct((16, 72, 384), BF),
            jax.ShapeDtypeStruct((16, 2, 3, 16, 128), BF),
        ),
        in_specs=[vmem, vmem, anyspace, anyspace, vmem],
        out_specs=(vmem, vmem),
        scratch_shapes=[
            pltpu.VMEM((1024, 1024), F32),
            pltpu.VMEM((2, 512, 1024), BF),
            pltpu.VMEM((2, 16, 2, 32, 512), BF),
            pltpu.VMEM((1024, 1536), BF),
            pltpu.VMEM((4, 4, 72, 384), BF),
            pltpu.VMEM((16, 2, 3, 16, 128), BF),
            pltpu.VMEM((16, 2, 2, 3, 16, 128), BF),
            pltpu.VMEM((128, 3, 4, 128), BF),
            pltpu.VMEM((128, 3, 4, 128), BF),
            pltpu.VMEM((16, 8, 3, 4, 128), BF),
            pltpu.VMEM((2, 128, 3, 4, 128), BF),
            pltpu.VMEM((16, 2, 3, 16, 128), BF),
            pltpu.VMEM((16, 2, 3, 16, 128), BF),
            pltpu.VMEM((4, 192, 384), BF),
            pltpu.VMEM((4, 192, 384), BF),
            pltpu.VMEM((192, 1536), BF),
            pltpu.VMEM((4, 288, 384), BF),
            *[dma] * 18,
            dma((4,)),
        ],
        compiler_params=pltpu.CompilerParams(
            collective_id=0, has_side_effects=True, vmem_limit_bytes=60 * 1024 * 1024
        ),
    )(volume, codes_in, x_transform, y_atoms, de)
    estimate = est.transpose(3, 0, 2, 1, 4).reshape(16, 48, 256)
    return (codes_out, estimate)


def solution(mesh):
    return jax.shard_map(
        shards,
        mesh=mesh,
        in_specs=(P("wide", None, "narrow"), P("wide", None, "narrow"), P(), P(), P()),
        out_specs=(P("wide", None, "narrow"), P("wide", None, "narrow")),
        check_vma=False,
    )
```

```python
import jax
import jax.numpy as jnp
from jax import lax
from jax.experimental import pallas as pl
from jax.experimental.pallas import tpu as pltpu
from jax.sharding import PartitionSpec as P

step_size = 0.06
threshold = 0.05
BF = jnp.bfloat16
F32 = jnp.float32
MESH = pl.DeviceIdType.MESH


def mm(a, b):
    return jnp.dot(a, b, preferred_element_type=F32)


def nt(a, b):
    return lax.dot_general(a, b, (((1,), (1,)), ((), ())), preferred_element_type=F32)


def tn(a, b):
    return lax.dot_general(a, b, (((0,), (0,)), ((), ())), preferred_element_type=F32)


def shrink(codes, grads):
    moved = codes - step_size * grads
    return (moved - jnp.clip(moved, -threshold, threshold)).astype(BF)


def remote(src, dst, send, recv, device):
    return pltpu.make_async_remote_copy(
        src_ref=src, dst_ref=dst, send_sem=send, recv_sem=recv, device_id=device, device_id_type=MESH
    )


def kernel(
    vol_in, codes, xin, din, de_in,
    new_low, new_high, est,
    vol, mine, new, de_small, de, xv, xrows, xcols, dv, codes4, send1, recv1, send2, recv2, send3, recv3, send4, recv4, qsend, qrecv, atoms, fresh,
    load, ssem1, rsem1, fsem1, gsem1, ssem2, rsem2, ssem3, rsem3, fsem3, gsem3, ssem4, rsem4,
    csend, crecv, qssem, qrsem, lsem,
):
    w = lax.axis_index("wide")
    n = lax.axis_index("narrow")
    half = n // 2
    core = n % 2
    chip = 2 * w + half
    twin = (w, 2 * half + 1 - core)
    bit = lax.rem(w // 2, 2)

    loads = [
        pltpu.make_async_copy(src, dst, load.at[i])
        for i, (src, dst) in enumerate(((vol_in, vol), (xin, xv), (de_in, de_small), (din, dv), (codes, mine)))
    ]
    load_vol, load_x, load_de, load_d, load_codes = loads
    for copy in loads:
        copy.start()

    barrier = pltpu.get_barrier_semaphore()

    def greet_from(i, c):
        frm = 4 * (i // 2) + 2 * (1 - core) + lax.rem(i, 2)
        pl.semaphore_signal(barrier, inc=1, device_id=(frm, 2 * half + bit), device_id_type=MESH)
        return c

    for d in (1, 2, 3):
        pl.semaphore_signal(barrier, inc=1, device_id=(w, lax.rem(n + d, 4)), device_id_type=MESH)
    lax.fori_loop(0, 32, greet_from, 0)

    load_vol.wait()
    for f in range(48):
        rows = vol[:, f, :].astype(BF)
        for b in range(2):
            send1[f // 3, b, f % 3] = rows[:, 128 * b : 128 * b + 128]

    pl.semaphore_wait(barrier, 35)

    def start1(i, c):
        t = lax.rem(w // 4 + i // 2, 16)
        b = lax.rem(w + i, 2)
        remote(
            send1.at[t, b], recv1.at[w // 4, bit, lax.rem(w, 2)], ssem1, rsem1, (4 * t + 2 * core + b, 2 * half + 1 - bit)
        ).start()
        return c

    lax.fori_loop(0, 32, start1, 0)
    for d in (2, 3, 1):
        other = lax.rem(n + d, 4)
        remote(
            codes.at[pl.ds(4 * other, 2)], codes4.at[n, 0:2], csend.at[0], crecv.at[0], (w, other)
        ).start()
    own_codes = pltpu.make_async_copy(codes.at[pl.ds(4 * n, 4)], codes4.at[n], lsem.at[0])
    own_codes.start()

    load_x.wait()

    def group_rows(i, c):
        rows = xv[pl.ds(pl.multiple_of(64 * i, 64), 64), :].reshape(8, 8, 1024)
        for s in range(2):
            xrows[s, pl.ds(pl.multiple_of(32 * i, 32), 32), :] = rows[:, 4 * s : 4 * s + 4].reshape(32, 1024).astype(BF)
        return c

    lax.fori_loop(0, 16, group_rows, 0)

    load_de.wait()
    spread = (lax.broadcasted_iota(jnp.int32, (192, 48), 0) // 4 == lax.broadcasted_iota(jnp.int32, (192, 48), 1))
    tile = (lax.rem(lax.broadcasted_iota(jnp.int32, (72, 288), 1), 72) == lax.broadcasted_iota(jnp.int32, (72, 288), 0))
    tall = mm(spread.astype(F32).astype(BF), de_small[...]).astype(BF)
    wide = mm(tall, tile.astype(F32).astype(BF))
    same = lax.rem(lax.broadcasted_iota(jnp.int32, (192, 288), 0), 4) == lax.broadcasted_iota(jnp.int32, (192, 288), 1) // 72
    de[...] = jnp.where(same, wide, 0.0).astype(BF)

    pltpu.make_async_copy(send1, recv1.at[:, 1 - core], rsem1).wait()
    for d in (2, 3, 1):
        other = lax.rem(n + d, 4)
        remote(
            codes.at[pl.ds(4 * other + 2, 2)], codes4.at[n, 2:4], csend.at[1], crecv.at[1], (w, other)
        ).start()
    forward = remote(recv1.at[:, 1 - core], recv1.at[:, 1 - core], fsem1, gsem1, twin)
    forward.start()
    pltpu.make_async_copy(send1, recv1.at[:, core], gsem1).wait()
    for f in range(3):
        mixed = mm(xrows[core], recv1[:, :, :, f].reshape(1024, 128))
        send2[:, f] = mixed.reshape(128, 4, 128).astype(BF)

    def start2(i, c):
        to = lax.rem(chip + 1 + i, 128)
        remote(send2.at[to], recv2.at[chip], ssem2, rsem2, (to // 2, 2 * lax.rem(to, 2) + core)).start()
        return c

    lax.fori_loop(0, 127, start2, 0)
    own2 = pltpu.make_async_copy(send2.at[chip], recv2.at[chip], lsem.at[1])
    own2.start()

    for s in range(2):

        def flip(i, c):
            part = xrows[s, :, pl.ds(pl.multiple_of(128 * i, 128), 128)].astype(F32)
            xcols[s, pl.ds(2 * i, 2)] = part.T.reshape(2, 2, 32, 512).astype(BF)
            return c

        lax.fori_loop(0, 8, flip, 0)

    load_d.wait()
    pltpu.make_async_copy(codes4.at[0:3, 0:2], codes4.at[0:3, 0:2], crecv.at[0]).wait()
    pltpu.make_async_copy(codes4.at[0:3, 2:4], codes4.at[0:3, 2:4], crecv.at[1]).wait()
    own_codes.wait()
    for m in range(4):
        atoms[:, 384 * m : 384 * m + 384] = mm(de[...], codes4[m].reshape(288, 384)).astype(BF)
    image = nt(atoms[...], dv[...])

    pltpu.make_async_copy(send2.at[0:127], recv2.at[0:127], rsem2).wait()
    own2.wait()
    got = recv2[...].reshape(16, 4, 2, 3, 4, 128)
    target = jnp.concatenate(
        [got[:, b, h].reshape(192, 128) for h in range(2) for b in range(4)], axis=1
    )
    misfit = (image - target.astype(F32)).astype(BF)
    for d in (2, 3, 1, 0):
        m = n ^ d
        q = mm(misfit, dv[:, pl.ds(pl.multiple_of(384 * m, 384), 384)]).astype(BF)
        qsend[m] = q
        if d:
            remote(qsend.at[m, 0:64], qrecv.at[n, 0:64], qssem.at[0], qrsem.at[0], (w, m)).start()
    for m in range(4):
        old = codes4[m].reshape(288, 384).astype(F32)
        fresh[m] = shrink(old, tn(de[...], qsend[m]))
    own_q = pltpu.make_async_copy(qsend.at[n], qrecv.at[n], lsem.at[2])
    own_q.start()
    for m in range(4):
        atoms[:, 384 * m : 384 * m + 384] = mm(de[...], fresh[m]).astype(BF)
    for h in range(2):
        for b in range(4):
            block = nt(atoms[...], dv[512 * h + 128 * b : 512 * h + 128 * b + 128, :])
            send3[:, 2 * b + h] = block.reshape(16, 3, 4, 128).astype(BF)

    def start3(i, c):
        to = lax.rem(chip + 1 + i, 128)
        remote(
            send3.at[to // 8, lax.rem(to, 8)], recv3.at[core, chip], ssem3, rsem3, (to // 2, 2 * lax.rem(to, 2) + core)
        ).start()
        return c

    lax.fori_loop(0, 127, start3, 0)
    own3 = pltpu.make_async_copy(send3.at[chip // 8, lax.rem(chip, 8)], recv3.at[core, chip], lsem.at[3])
    own3.start()
    pltpu.make_async_copy(send2.at[0:127], recv3.at[core, 0:127], rsem3).wait()
    for d in (2, 3, 1):
        other = lax.rem(n + d, 4)
        remote(qsend.at[other, 64:192], qrecv.at[n, 64:192], qssem.at[1], qrsem.at[1], (w, other)).start()
    own3.wait()
    forward3 = remote(recv3.at[core], recv3.at[core], fsem3, gsem3, twin)
    forward3.start()
    pltpu.make_async_copy(send2, recv3.at[1 - core], gsem3).wait()

    for f in range(3):
        back = mm(xcols[0, :, 1 - core].reshape(512, 512), recv3[0, :, f].reshape(512, 128))
        back += mm(xcols[1, :, 1 - core].reshape(512, 512), recv3[1, :, f].reshape(512, 128))
        send4[:, :, f] = jnp.maximum(back, 0.0).reshape(16, 2, 16, 128).astype(BF)

    def start4(i, c):
        a = lax.rem(w // 4 + i // 2, 16)
        b = lax.rem(w + i, 2)
        to = 4 * a + 2 * (1 - core) + b
        remote(send4.at[a, b], recv4.at[w // 4, lax.rem(w, 2)], ssem4, rsem4, (to, 2 * half + bit)).start()
        return c

    lax.fori_loop(0, 32, start4, 0)

    pltpu.make_async_copy(qsend.at[0:3, 0:64], qrecv.at[0:3, 0:64], qrsem.at[0]).wait()
    pltpu.make_async_copy(qsend.at[0:3, 64:192], qrecv.at[0:3, 64:192], qrsem.at[1]).wait()
    load_codes.wait()
    own_q.wait()
    for m in range(4):
        old = mine[4 * m : 4 * m + 4].reshape(288, 384).astype(F32)
        new[4 * m : 4 * m + 4] = shrink(old, tn(de[...], qrecv[m])).reshape(4, 72, 384)

    put_low = pltpu.make_async_copy(new.at[0:8], new_low, lsem.at[4])
    put_high = pltpu.make_async_copy(new.at[8:16], new_high, lsem.at[6])
    put_low.start()
    put_high.start()
    pltpu.make_async_copy(send4, recv4, rsem4).wait()
    put_est = pltpu.make_async_copy(recv4, est, lsem.at[5])
    put_est.start()

    pltpu.make_async_copy(send1, send1, ssem1).wait()
    pltpu.make_async_copy(send1, send1, fsem1).wait()
    pltpu.make_async_copy(send2.at[0:127], send2.at[0:127], ssem2).wait()
    pltpu.make_async_copy(send2.at[0:127], send2.at[0:127], ssem3).wait()
    pltpu.make_async_copy(send2, send2, fsem3).wait()
    pltpu.make_async_copy(send4, send4, ssem4).wait()
    pltpu.make_async_copy(codes4.at[0:3, 0:2], codes4.at[0:3, 0:2], csend.at[0]).wait()
    pltpu.make_async_copy(codes4.at[0:3, 2:4], codes4.at[0:3, 2:4], csend.at[1]).wait()
    pltpu.make_async_copy(qsend.at[0:3, 0:64], qsend.at[0:3, 0:64], qssem.at[0]).wait()
    pltpu.make_async_copy(qsend.at[0:3, 64:192], qsend.at[0:3, 64:192], qssem.at[1]).wait()
    put_low.wait()
    put_high.wait()
    put_est.wait()


def finish(low, high, est, codes_out, estimate, flat, out, sem):
    put_low = pltpu.make_async_copy(low, codes_out.at[0:8], sem.at[0])
    put_high = pltpu.make_async_copy(high, codes_out.at[8:16], sem.at[2])
    put_low.start()
    put_high.start()
    for b in range(2):
        for f in range(48):
            flat[:, f] = est[f // 3, b, f % 3].astype(F32)
        out[:, :, 128 * b : 128 * b + 128] = flat[...].astype(BF)
    put_est = pltpu.make_async_copy(out, estimate, sem.at[1])
    put_est.start()
    put_low.wait()
    put_high.wait()
    put_est.wait()


def shards(volume, codes_in, x_transform, y_atoms, de_atoms):
    dma = pltpu.SemaphoreType.DMA
    anyspace = pl.BlockSpec(memory_space=pl.ANY)
    low, high, est = pl.pallas_call(
        kernel,
        out_shape=(
            jax.ShapeDtypeStruct((8, 72, 384), BF),
            jax.ShapeDtypeStruct((8, 72, 384), BF),
            jax.ShapeDtypeStruct((16, 2, 3, 16, 128), BF),
        ),
        in_specs=[anyspace] * 5,
        out_specs=(anyspace, anyspace, anyspace),
        scratch_shapes=[
            pltpu.VMEM((16, 48, 256), F32),
            pltpu.VMEM((16, 72, 384), BF),
            pltpu.VMEM((16, 72, 384), BF),
            pltpu.VMEM((48, 72), BF),
            pltpu.VMEM((192, 288), BF),
            pltpu.VMEM((1024, 1024), F32),
            pltpu.VMEM((2, 512, 1024), BF),
            pltpu.VMEM((2, 16, 2, 32, 512), BF),
            pltpu.VMEM((1024, 1536), BF),
            pltpu.VMEM((4, 4, 72, 384), BF),
            pltpu.VMEM((16, 2, 3, 16, 128), BF),
            pltpu.VMEM((16, 2, 2, 3, 16, 128), BF),
            pltpu.VMEM((128, 3, 4, 128), BF),
            pltpu.VMEM((128, 3, 4, 128), BF),
            pltpu.VMEM((16, 8, 3, 4, 128), BF),
            pltpu.VMEM((2, 128, 3, 4, 128), BF),
            pltpu.VMEM((16, 2, 3, 16, 128), BF),
            pltpu.VMEM((16, 2, 3, 16, 128), BF),
            pltpu.VMEM((4, 192, 384), BF),
            pltpu.VMEM((4, 192, 384), BF),
            pltpu.VMEM((192, 1536), BF),
            pltpu.VMEM((4, 288, 384), BF),
            dma((5,)),
            *[dma] * 12,
            *[dma((2,))] * 4,
            dma((7,)),
        ],
        compiler_params=pltpu.CompilerParams(
            collective_id=0, has_side_effects=True, vmem_limit_bytes=54850000
        ),
    )(volume, codes_in, x_transform, y_atoms, de_atoms)
    return pl.pallas_call(
        finish,
        out_shape=(
            jax.ShapeDtypeStruct((16, 72, 384), BF),
            jax.ShapeDtypeStruct((16, 48, 256), BF),
        ),
        in_specs=[pl.BlockSpec(memory_space=pltpu.VMEM)] * 3,
        out_specs=(anyspace, anyspace),
        scratch_shapes=[
            pltpu.VMEM((16, 48, 128), F32),
            pltpu.VMEM((16, 48, 256), BF),
            dma((3,)),
        ],
        compiler_params=pltpu.CompilerParams(vmem_limit_bytes=8 * 1024 * 1024),
    )(low, high, est)


def solution(mesh):
    return jax.shard_map(
        shards,
        mesh=mesh,
        in_specs=(P("wide", None, "narrow"), P("wide", None, "narrow"), P(), P(), P()),
        out_specs=(P("wide", None, "narrow"), P("wide", None, "narrow")),
        check_vma=False,
    )
```

```python
import jax
import jax.numpy as jnp
from jax import lax
from jax.experimental import pallas as pl
from jax.experimental.pallas import tpu as pltpu
from jax.sharding import PartitionSpec as P

step_size = 0.06
threshold = 0.05
BF = jnp.bfloat16
F32 = jnp.float32
MESH = pl.DeviceIdType.MESH


def mm(a, b):
    return jnp.dot(a, b, preferred_element_type=F32)


def nt(a, b):
    return lax.dot_general(a, b, (((1,), (1,)), ((), ())), preferred_element_type=F32)


def tn(a, b):
    return lax.dot_general(a, b, (((0,), (0,)), ((), ())), preferred_element_type=F32)


def shrink(codes, grads):
    moved = codes - step_size * grads
    return (moved - jnp.clip(moved, -threshold, threshold)).astype(BF)


def remote(src, dst, send, recv, device):
    return pltpu.make_async_remote_copy(
        src_ref=src, dst_ref=dst, send_sem=send, recv_sem=recv, device_id=device, device_id_type=MESH
    )


def kernel(
    vol_in, codes, xin, din, de_in,
    new_low, new_high, est,
    vol, mine, new, de_small, de, xv, xrows, xcols, dv, codes4, send1, recv1, send2, recv2, send3, recv3, send4, recv4, qsend, qrecv, atoms, fresh,
    load, ssem1, rsem1, fsem1, gsem1, ssem2, rsem2, ssem3, rsem3, fsem3, gsem3, ssem4, rsem4,
    csend, crecv, qssem, qrsem, lsem, msem, relays, mid, midq,
):
    w = lax.axis_index("wide")
    n = lax.axis_index("narrow")
    half = n // 2
    core = n % 2
    chip = 2 * w + half
    twin = (w, 2 * half + 1 - core)
    bit = lax.rem(w // 2, 2)
    low = lax.rem(w, 4)
    across = w - low + lax.rem(low + 2, 4)
    up_half = lax.rem(half + low // 2, 2)
    down_half = 1 - up_half
    up = (across, 2 * up_half + core)
    down = (across, 2 * down_half + core)
    down_other = (across, 2 * down_half + 1 - core)
    near = n + 1 - 2 * core
    facing = lax.rem(n + 2, 4)
    cross = 2 * (1 - half) + 1 - core

    loads = [
        pltpu.make_async_copy(src, dst, load.at[i])
        for i, (src, dst) in enumerate(((vol_in, vol), (xin, xv), (de_in, de_small), (din, dv), (codes, mine)))
    ]
    load_vol, load_x, load_de, load_d, load_codes = loads
    for copy in loads:
        copy.start()

    barrier = pltpu.get_barrier_semaphore()

    def greet_from(i, c):
        frm = 4 * (i // 2) + 2 * (1 - core) + lax.rem(i, 2)
        pl.semaphore_signal(barrier, inc=1, device_id=(frm, 2 * half + bit), device_id_type=MESH)
        return c

    for d in (1, 2, 3):
        pl.semaphore_signal(barrier, inc=1, device_id=(w, lax.rem(n + d, 4)), device_id_type=MESH)
    for to in (up, down, (across, 2 * up_half + 1 - core)):
        pl.semaphore_signal(barrier, inc=1, device_id=to, device_id_type=MESH)
    lax.fori_loop(0, 32, greet_from, 0)

    load_vol.wait()
    for f in range(48):
        rows = vol[:, f, :].astype(BF)
        for b in range(2):
            send1[f // 3, b, f % 3] = rows[:, 128 * b : 128 * b + 128]

    pl.semaphore_wait(barrier, 38)

    def start1(i, c):
        t = lax.rem(w // 4 + i // 2, 16)
        b = lax.rem(w + i, 2)
        remote(
            send1.at[t, b], recv1.at[w // 4, bit, lax.rem(w, 2)], ssem1, rsem1, (4 * t + 2 * core + b, 2 * half + 1 - bit)
        ).start()
        return c

    lax.fori_loop(0, 32, start1, 0)
    remote(codes.at[4 * facing + 0], mid.at[0, 0], csend.at[0], msem.at[0, 0], up).start()
    remote(codes.at[4 * cross + 0], mid.at[1, 0], csend.at[0], msem.at[1, 0], down).start()
    remote(codes.at[4 * facing + 1], mid.at[0, 1], csend.at[0], msem.at[0, 1], up).start()
    remote(codes.at[4 * cross + 1], mid.at[1, 1], csend.at[0], msem.at[1, 1], down).start()
    remote(codes.at[4 * facing + 2], mid.at[0, 2], csend.at[0], msem.at[0, 2], up).start()
    remote(codes.at[4 * cross + 2], mid.at[1, 2], csend.at[0], msem.at[1, 2], down).start()
    remote(codes.at[pl.ds(4 * near + 0, 3)], codes4.at[n, 0:3], csend.at[0], crecv.at[0], (w, near)).start()
    own_codes = pltpu.make_async_copy(codes.at[pl.ds(4 * n, 4)], codes4.at[n], lsem.at[0])
    own_codes.start()

    load_x.wait()

    def group_rows(i, c):
        rows = xv[pl.ds(pl.multiple_of(64 * i, 64), 64), :].reshape(8, 8, 1024)
        for s in range(2):
            xrows[s, pl.ds(pl.multiple_of(32 * i, 32), 32), :] = rows[:, 4 * s : 4 * s + 4].reshape(32, 1024).astype(BF)
        return c

    lax.fori_loop(0, 16, group_rows, 0)

    load_de.wait()
    spread = (lax.broadcasted_iota(jnp.int32, (192, 48), 0) // 4 == lax.broadcasted_iota(jnp.int32, (192, 48), 1))
    tile = (lax.rem(lax.broadcasted_iota(jnp.int32, (72, 288), 1), 72) == lax.broadcasted_iota(jnp.int32, (72, 288), 0))
    tall = mm(spread.astype(F32).astype(BF), de_small[...]).astype(BF)
    wide = mm(tall, tile.astype(F32).astype(BF))
    same = lax.rem(lax.broadcasted_iota(jnp.int32, (192, 288), 0), 4) == lax.broadcasted_iota(jnp.int32, (192, 288), 1) // 72
    de[...] = jnp.where(same, wide, 0.0).astype(BF)

    pltpu.make_async_copy(mid.at[0, 0], mid.at[0, 0], msem.at[0, 0]).wait()
    remote(mid.at[0, 0], codes4.at[2 * down_half + core, 0], relays.at[0], crecv.at[0], up).start()
    pltpu.make_async_copy(mid.at[1, 0], mid.at[1, 0], msem.at[1, 0]).wait()
    remote(mid.at[1, 0], codes4.at[2 * up_half + core, 0], relays.at[0], crecv.at[0], down_other).start()
    pltpu.make_async_copy(mid.at[0, 1], mid.at[0, 1], msem.at[0, 1]).wait()
    remote(mid.at[0, 1], codes4.at[2 * down_half + core, 1], relays.at[0], crecv.at[0], up).start()
    pltpu.make_async_copy(mid.at[1, 1], mid.at[1, 1], msem.at[1, 1]).wait()
    remote(mid.at[1, 1], codes4.at[2 * up_half + core, 1], relays.at[0], crecv.at[0], down_other).start()
    pltpu.make_async_copy(mid.at[0, 2], mid.at[0, 2], msem.at[0, 2]).wait()
    remote(mid.at[0, 2], codes4.at[2 * down_half + core, 2], relays.at[0], crecv.at[0], up).start()
    pltpu.make_async_copy(mid.at[1, 2], mid.at[1, 2], msem.at[1, 2]).wait()
    remote(mid.at[1, 2], codes4.at[2 * up_half + core, 2], relays.at[0], crecv.at[0], down_other).start()
    pltpu.make_async_copy(send1, recv1.at[:, 1 - core], rsem1).wait()
    forward = remote(recv1.at[:, 1 - core], recv1.at[:, 1 - core], fsem1, gsem1, twin)
    forward.start()
    remote(codes.at[4 * facing + 3], mid.at[0, 3], csend.at[1], msem.at[0, 3], up).start()
    remote(codes.at[4 * cross + 3], mid.at[1, 3], csend.at[1], msem.at[1, 3], down).start()
    remote(codes.at[pl.ds(4 * near + 3, 1)], codes4.at[n, 3:4], csend.at[1], crecv.at[1], (w, near)).start()
    pltpu.make_async_copy(send1, recv1.at[:, core], gsem1).wait()
    for f in range(3):
        mixed = mm(xrows[core], recv1[:, :, :, f].reshape(1024, 128))
        send2[:, f] = mixed.reshape(128, 4, 128).astype(BF)

    def start2(i, c):
        to = lax.rem(chip + 1 + i, 128)
        remote(send2.at[to], recv2.at[chip], ssem2, rsem2, (to // 2, 2 * lax.rem(to, 2) + core)).start()
        return c

    lax.fori_loop(0, 127, start2, 0)
    own2 = pltpu.make_async_copy(send2.at[chip], recv2.at[chip], lsem.at[1])
    own2.start()
    pltpu.make_async_copy(mid.at[0, 3], mid.at[0, 3], msem.at[0, 3]).wait()
    remote(mid.at[0, 3], codes4.at[2 * down_half + core, 3], relays.at[0], crecv.at[1], up).start()
    pltpu.make_async_copy(mid.at[1, 3], mid.at[1, 3], msem.at[1, 3]).wait()
    remote(mid.at[1, 3], codes4.at[2 * up_half + core, 3], relays.at[0], crecv.at[1], down_other).start()

    for s in range(2):

        def flip(i, c):
            part = xrows[s, :, pl.ds(pl.multiple_of(128 * i, 128), 128)].astype(F32)
            xcols[s, pl.ds(2 * i, 2)] = part.T.reshape(2, 2, 32, 512).astype(BF)
            return c

        lax.fori_loop(0, 8, flip, 0)

    load_d.wait()
    pltpu.make_async_copy(codes4.at[0:3, 0:3], codes4.at[0:3, 0:3], crecv.at[0]).wait()
    pltpu.make_async_copy(codes4.at[0:3, 3:4], codes4.at[0:3, 3:4], crecv.at[1]).wait()
    own_codes.wait()
    for m in range(4):
        atoms[:, 384 * m : 384 * m + 384] = mm(de[...], codes4[m].reshape(288, 384)).astype(BF)
    image = nt(atoms[...], dv[...])

    pltpu.make_async_copy(send2.at[0:127], recv2.at[0:127], rsem2).wait()
    own2.wait()
    got = recv2[...].reshape(16, 4, 2, 3, 4, 128)
    target = jnp.concatenate(
        [got[:, b, h].reshape(192, 128) for h in range(2) for b in range(4)], axis=1
    )
    misfit = (image - target.astype(F32)).astype(BF)
    for d in (2, 3, 1, 0):
        m = n ^ d
        q = mm(misfit, dv[:, pl.ds(pl.multiple_of(384 * m, 384), 384)]).astype(BF)
        qsend[m] = q
        if d == 2:
            remote(qsend.at[m, 0:128], midq.at[0, 0:128], qssem.at[0], msem.at[0, 4], up).start()
        elif d == 3:
            remote(qsend.at[m, 0:128], midq.at[1, 0:128], qssem.at[0], msem.at[1, 4], down).start()
        elif d == 1:
            remote(qsend.at[m, 0:128], qrecv.at[n, 0:128], qssem.at[0], qrsem.at[0], (w, m)).start()
    for m in range(4):
        old = codes4[m].reshape(288, 384).astype(F32)
        fresh[m] = shrink(old, tn(de[...], qsend[m]))
    own_q = pltpu.make_async_copy(qsend.at[n], qrecv.at[n], lsem.at[2])
    own_q.start()
    for m in range(4):
        atoms[:, 384 * m : 384 * m + 384] = mm(de[...], fresh[m]).astype(BF)
    for h in range(2):
        for b in range(4):
            block = nt(atoms[...], dv[512 * h + 128 * b : 512 * h + 128 * b + 128, :])
            send3[:, 2 * b + h] = block.reshape(16, 3, 4, 128).astype(BF)

    def start3(i, c):
        to = lax.rem(chip + 1 + i, 128)
        remote(
            send3.at[to // 8, lax.rem(to, 8)], recv3.at[core, chip], ssem3, rsem3, (to // 2, 2 * lax.rem(to, 2) + core)
        ).start()
        return c

    lax.fori_loop(0, 127, start3, 0)
    own3 = pltpu.make_async_copy(send3.at[chip // 8, lax.rem(chip, 8)], recv3.at[core, chip], lsem.at[3])
    own3.start()
    pltpu.make_async_copy(midq.at[0, 0:128], midq.at[0, 0:128], msem.at[0, 4]).wait()
    remote(midq.at[0, 0:128], qrecv.at[2 * down_half + core, 0:128], relays.at[1], qrsem.at[0], up).start()
    pltpu.make_async_copy(midq.at[1, 0:128], midq.at[1, 0:128], msem.at[1, 4]).wait()
    remote(midq.at[1, 0:128], qrecv.at[2 * up_half + core, 0:128], relays.at[1], qrsem.at[0], down_other).start()
    pltpu.make_async_copy(send2.at[0:127], recv3.at[core, 0:127], rsem3).wait()
    own3.wait()
    forward3 = remote(recv3.at[core], recv3.at[core], fsem3, gsem3, twin)
    forward3.start()
    remote(qsend.at[facing, 128:160], midq.at[0, 128:160], qssem.at[1], msem.at[0, 5], up).start()
    remote(qsend.at[cross, 128:160], midq.at[1, 128:160], qssem.at[1], msem.at[1, 5], down).start()
    remote(qsend.at[facing, 160:192], midq.at[0, 160:192], qssem.at[1], msem.at[0, 6], up).start()
    remote(qsend.at[cross, 160:192], midq.at[1, 160:192], qssem.at[1], msem.at[1, 6], down).start()
    remote(qsend.at[near, 128:192], qrecv.at[n, 128:192], qssem.at[1], qrsem.at[1], (w, near)).start()
    pltpu.make_async_copy(send2, recv3.at[1 - core], gsem3).wait()

    for f in range(3):
        back = mm(xcols[0, :, 1 - core].reshape(512, 512), recv3[0, :, f].reshape(512, 128))
        back += mm(xcols[1, :, 1 - core].reshape(512, 512), recv3[1, :, f].reshape(512, 128))
        send4[:, :, f] = jnp.maximum(back, 0.0).reshape(16, 2, 16, 128).astype(BF)

    def start4(i, c):
        a = lax.rem(w // 4 + i // 2, 16)
        b = lax.rem(w + i, 2)
        to = 4 * a + 2 * (1 - core) + b
        remote(send4.at[a, b], recv4.at[w // 4, lax.rem(w, 2)], ssem4, rsem4, (to, 2 * half + bit)).start()
        return c

    lax.fori_loop(0, 32, start4, 0)
    pltpu.make_async_copy(midq.at[0, 128:160], midq.at[0, 128:160], msem.at[0, 5]).wait()
    remote(midq.at[0, 128:160], qrecv.at[2 * down_half + core, 128:160], relays.at[1], qrsem.at[1], up).start()
    pltpu.make_async_copy(midq.at[1, 128:160], midq.at[1, 128:160], msem.at[1, 5]).wait()
    remote(midq.at[1, 128:160], qrecv.at[2 * up_half + core, 128:160], relays.at[1], qrsem.at[1], down_other).start()
    pltpu.make_async_copy(midq.at[0, 160:192], midq.at[0, 160:192], msem.at[0, 6]).wait()
    remote(midq.at[0, 160:192], qrecv.at[2 * down_half + core, 160:192], relays.at[1], qrsem.at[1], up).start()
    pltpu.make_async_copy(midq.at[1, 160:192], midq.at[1, 160:192], msem.at[1, 6]).wait()
    remote(midq.at[1, 160:192], qrecv.at[2 * up_half + core, 160:192], relays.at[1], qrsem.at[1], down_other).start()

    pltpu.make_async_copy(qsend.at[0:3, 0:128], qrecv.at[0:3, 0:128], qrsem.at[0]).wait()
    pltpu.make_async_copy(qsend.at[0:3, 128:192], qrecv.at[0:3, 128:192], qrsem.at[1]).wait()
    load_codes.wait()
    own_q.wait()
    for m in range(4):
        old = mine[4 * m : 4 * m + 4].reshape(288, 384).astype(F32)
        new[4 * m : 4 * m + 4] = shrink(old, tn(de[...], qrecv[m])).reshape(4, 72, 384)

    put_low = pltpu.make_async_copy(new.at[0:8], new_low, lsem.at[4])
    put_high = pltpu.make_async_copy(new.at[8:16], new_high, lsem.at[6])
    put_low.start()
    put_high.start()
    pltpu.make_async_copy(send4, recv4, rsem4).wait()
    put_est = pltpu.make_async_copy(recv4, est, lsem.at[5])
    put_est.start()

    pltpu.make_async_copy(send1, send1, ssem1).wait()
    pltpu.make_async_copy(send1, send1, fsem1).wait()
    pltpu.make_async_copy(send2.at[0:127], send2.at[0:127], ssem2).wait()
    pltpu.make_async_copy(send2.at[0:127], send2.at[0:127], ssem3).wait()
    pltpu.make_async_copy(send2, send2, fsem3).wait()
    pltpu.make_async_copy(send4, send4, ssem4).wait()
    pltpu.make_async_copy(codes4.at[0:3, 0:3], codes4.at[0:3, 0:3], csend.at[0]).wait()
    pltpu.make_async_copy(codes4.at[0:3, 3:4], codes4.at[0:3, 3:4], csend.at[1]).wait()
    pltpu.make_async_copy(qsend.at[0:3, 0:128], qsend.at[0:3, 0:128], qssem.at[0]).wait()
    pltpu.make_async_copy(qsend.at[0:3, 128:192], qsend.at[0:3, 128:192], qssem.at[1]).wait()
    pltpu.make_async_copy(mid, mid, relays.at[0]).wait()
    pltpu.make_async_copy(midq, midq, relays.at[1]).wait()
    put_low.wait()
    put_high.wait()
    put_est.wait()


def finish(low, high, est, codes_out, estimate, flat, out, sem):
    put_low = pltpu.make_async_copy(low, codes_out.at[0:8], sem.at[0])
    put_high = pltpu.make_async_copy(high, codes_out.at[8:16], sem.at[2])
    put_low.start()
    put_high.start()
    for b in range(2):
        for f in range(48):
            flat[:, f] = est[f // 3, b, f % 3].astype(F32)
        out[:, :, 128 * b : 128 * b + 128] = flat[...].astype(BF)
    put_est = pltpu.make_async_copy(out, estimate, sem.at[1])
    put_est.start()
    put_low.wait()
    put_high.wait()
    put_est.wait()


def shards(volume, codes_in, x_transform, y_atoms, de_atoms):
    dma = pltpu.SemaphoreType.DMA
    anyspace = pl.BlockSpec(memory_space=pl.ANY)
    low, high, est = pl.pallas_call(
        kernel,
        out_shape=(
            jax.ShapeDtypeStruct((8, 72, 384), BF),
            jax.ShapeDtypeStruct((8, 72, 384), BF),
            jax.ShapeDtypeStruct((16, 2, 3, 16, 128), BF),
        ),
        in_specs=[anyspace] * 5,
        out_specs=(anyspace, anyspace, anyspace),
        scratch_shapes=[
            pltpu.VMEM((16, 48, 256), F32),
            pltpu.VMEM((16, 72, 384), BF),
            pltpu.VMEM((16, 72, 384), BF),
            pltpu.VMEM((48, 72), BF),
            pltpu.VMEM((192, 288), BF),
            pltpu.VMEM((1024, 1024), F32),
            pltpu.VMEM((2, 512, 1024), BF),
            pltpu.VMEM((2, 16, 2, 32, 512), BF),
            pltpu.VMEM((1024, 1536), BF),
            pltpu.VMEM((4, 4, 72, 384), BF),
            pltpu.VMEM((16, 2, 3, 16, 128), BF),
            pltpu.VMEM((16, 2, 2, 3, 16, 128), BF),
            pltpu.VMEM((128, 3, 4, 128), BF),
            pltpu.VMEM((128, 3, 4, 128), BF),
            pltpu.VMEM((16, 8, 3, 4, 128), BF),
            pltpu.VMEM((2, 128, 3, 4, 128), BF),
            pltpu.VMEM((16, 2, 3, 16, 128), BF),
            pltpu.VMEM((16, 2, 3, 16, 128), BF),
            pltpu.VMEM((4, 192, 384), BF),
            pltpu.VMEM((4, 192, 384), BF),
            pltpu.VMEM((192, 1536), BF),
            pltpu.VMEM((4, 288, 384), BF),
            dma((5,)),
            *[dma] * 12,
            *[dma((2,))] * 4,
            dma((7,)),
            dma((2, 7)),
            dma((2,)),
            pltpu.VMEM((2, 4, 72, 384), BF),
            pltpu.VMEM((2, 192, 384), BF),
        ],
        compiler_params=pltpu.CompilerParams(
            collective_id=0, has_side_effects=True, vmem_limit_bytes=54850000
        ),
    )(volume, codes_in, x_transform, y_atoms, de_atoms)
    return pl.pallas_call(
        finish,
        out_shape=(
            jax.ShapeDtypeStruct((16, 72, 384), BF),
            jax.ShapeDtypeStruct((16, 48, 256), BF),
        ),
        in_specs=[pl.BlockSpec(memory_space=pltpu.VMEM)] * 3,
        out_specs=(anyspace, anyspace),
        scratch_shapes=[
            pltpu.VMEM((16, 48, 128), F32),
            pltpu.VMEM((16, 48, 256), BF),
            dma((3,)),
        ],
        compiler_params=pltpu.CompilerParams(vmem_limit_bytes=8 * 1024 * 1024),
    )(low, high, est)


def solution(mesh):
    return jax.shard_map(
        shards,
        mesh=mesh,
        in_specs=(P("wide", None, "narrow"), P("wide", None, "narrow"), P(), P(), P()),
        out_specs=(P("wide", None, "narrow"), P("wide", None, "narrow")),
        check_vma=False,
    )
```

```python
import jax
import jax.numpy as jnp
from jax import lax
from jax.experimental import pallas as pl
from jax.experimental.pallas import tpu as pltpu
from jax.sharding import PartitionSpec as P

step_size = 0.06
threshold = 0.05
BF = jnp.bfloat16
F32 = jnp.float32
MESH = pl.DeviceIdType.MESH


def mm(a, b):
    return jnp.dot(a, b, preferred_element_type=F32)


def nt(a, b):
    return lax.dot_general(a, b, (((1,), (1,)), ((), ())), preferred_element_type=F32)


def tn(a, b):
    return lax.dot_general(a, b, (((0,), (0,)), ((), ())), preferred_element_type=F32)


def shrink(codes, grads):
    moved = codes - step_size * grads
    return (moved - jnp.clip(moved, -threshold, threshold)).astype(BF)


def remote(src, dst, send, recv, device):
    return pltpu.make_async_remote_copy(
        src_ref=src, dst_ref=dst, send_sem=send, recv_sem=recv, device_id=device, device_id_type=MESH
    )


def kernel(
    vol_in, codes, xin, din, de_in,
    new_low, new_high, est,
    vol, mine, new, de_small, de, xv, xrows, xcols, dv, codes4, send1, recv1, send2, recv2, send3, recv3, send4, recv4, qsend, qrecv, atoms, fresh,
    load, ssem1, rsem1, fsem1, gsem1, ssem2, rsem2, ssem3, rsem3, fsem3, gsem3, ssem4, rsem4,
    csend, crecv, qssem, qrsem, lsem, msem, relays, mid, midq,
):
    w = lax.axis_index("wide")
    n = lax.axis_index("narrow")
    half = n // 2
    core = n % 2
    chip = 2 * w + half
    twin = (w, 2 * half + 1 - core)
    bit = lax.rem(w // 2, 2)
    low = lax.rem(w, 4)
    across = w - low + lax.rem(low + 2, 4)
    up_half = lax.rem(half + low // 2, 2)
    down_half = 1 - up_half
    up = (across, 2 * up_half + core)
    down = (across, 2 * down_half + core)
    down_other = (across, 2 * down_half + 1 - core)
    near = n + 1 - 2 * core
    facing = lax.rem(n + 2, 4)
    cross = 2 * (1 - half) + 1 - core

    loads = [
        pltpu.make_async_copy(src, dst, load.at[i])
        for i, (src, dst) in enumerate(((vol_in, vol), (xin, xv), (de_in, de_small), (din, dv), (codes, mine)))
    ]
    load_vol, load_x, load_de, load_d, load_codes = loads
    load_vol.start()

    barrier = pltpu.get_barrier_semaphore()

    def greet_from(i, c):
        frm = 4 * (i // 2) + 2 * (1 - core) + lax.rem(i, 2)
        pl.semaphore_signal(barrier, inc=1, device_id=(frm, 2 * half + bit), device_id_type=MESH)
        return c

    for d in (1, 2, 3):
        pl.semaphore_signal(barrier, inc=1, device_id=(w, lax.rem(n + d, 4)), device_id_type=MESH)
    for to in (up, down, (across, 2 * up_half + 1 - core)):
        pl.semaphore_signal(barrier, inc=1, device_id=to, device_id_type=MESH)
    lax.fori_loop(0, 32, greet_from, 0)

    for copy in loads[1:]:
        copy.start()
    load_vol.wait()
    for f in range(48):
        rows = vol[:, f, :].astype(BF)
        for b in range(2):
            send1[f // 3, b, f % 3] = rows[:, 128 * b : 128 * b + 128]

    pl.semaphore_wait(barrier, 38)

    def start1(i, c):
        t = lax.rem(w // 4 + i // 2, 16)
        b = lax.rem(w + i, 2)
        remote(
            send1.at[t, b], recv1.at[w // 4, bit, lax.rem(w, 2)], ssem1, rsem1, (4 * t + 2 * core + b, 2 * half + 1 - bit)
        ).start()
        return c

    lax.fori_loop(0, 32, start1, 0)
    remote(codes.at[4 * facing + 0], mid.at[0, 0], csend.at[0], msem.at[0, 0], up).start()
    remote(codes.at[4 * cross + 0], mid.at[1, 0], csend.at[0], msem.at[1, 0], down).start()
    remote(codes.at[4 * facing + 1], mid.at[0, 1], csend.at[0], msem.at[0, 1], up).start()
    remote(codes.at[4 * cross + 1], mid.at[1, 1], csend.at[0], msem.at[1, 1], down).start()
    remote(codes.at[4 * facing + 2], mid.at[0, 2], csend.at[0], msem.at[0, 2], up).start()
    remote(codes.at[4 * cross + 2], mid.at[1, 2], csend.at[0], msem.at[1, 2], down).start()
    remote(codes.at[pl.ds(4 * near + 0, 3)], codes4.at[n, 0:3], csend.at[0], crecv.at[0], (w, near)).start()
    remote(codes.at[4 * facing + 3], mid.at[0, 3], csend.at[1], msem.at[0, 3], up).start()
    remote(codes.at[4 * cross + 3], mid.at[1, 3], csend.at[1], msem.at[1, 3], down).start()
    remote(codes.at[pl.ds(4 * near + 3, 1)], codes4.at[n, 3:4], csend.at[1], crecv.at[1], (w, near)).start()
    own_codes = pltpu.make_async_copy(codes.at[pl.ds(4 * n, 4)], codes4.at[n], lsem.at[0])
    own_codes.start()

    load_x.wait()

    def group_rows(i, c):
        rows = xv[pl.ds(pl.multiple_of(64 * i, 64), 64), :].reshape(8, 8, 1024)
        for s in range(2):
            xrows[s, pl.ds(pl.multiple_of(32 * i, 32), 32), :] = rows[:, 4 * s : 4 * s + 4].reshape(32, 1024).astype(BF)
        return c

    lax.fori_loop(0, 16, group_rows, 0)

    load_de.wait()
    spread = (lax.broadcasted_iota(jnp.int32, (192, 48), 0) // 4 == lax.broadcasted_iota(jnp.int32, (192, 48), 1))
    tile = (lax.rem(lax.broadcasted_iota(jnp.int32, (72, 288), 1), 72) == lax.broadcasted_iota(jnp.int32, (72, 288), 0))
    tall = mm(spread.astype(F32).astype(BF), de_small[...]).astype(BF)
    wide = mm(tall, tile.astype(F32).astype(BF))
    same = lax.rem(lax.broadcasted_iota(jnp.int32, (192, 288), 0), 4) == lax.broadcasted_iota(jnp.int32, (192, 288), 1) // 72
    de[...] = jnp.where(same, wide, 0.0).astype(BF)

    pltpu.make_async_copy(mid.at[0, 0], mid.at[0, 0], msem.at[0, 0]).wait()
    remote(mid.at[0, 0], codes4.at[2 * down_half + core, 0], relays.at[0], crecv.at[0], up).start()
    pltpu.make_async_copy(mid.at[1, 0], mid.at[1, 0], msem.at[1, 0]).wait()
    remote(mid.at[1, 0], codes4.at[2 * up_half + core, 0], relays.at[0], crecv.at[0], down_other).start()
    pltpu.make_async_copy(mid.at[0, 1], mid.at[0, 1], msem.at[0, 1]).wait()
    remote(mid.at[0, 1], codes4.at[2 * down_half + core, 1], relays.at[0], crecv.at[0], up).start()
    pltpu.make_async_copy(mid.at[1, 1], mid.at[1, 1], msem.at[1, 1]).wait()
    remote(mid.at[1, 1], codes4.at[2 * up_half + core, 1], relays.at[0], crecv.at[0], down_other).start()
    pltpu.make_async_copy(mid.at[0, 2], mid.at[0, 2], msem.at[0, 2]).wait()
    remote(mid.at[0, 2], codes4.at[2 * down_half + core, 2], relays.at[0], crecv.at[0], up).start()
    pltpu.make_async_copy(mid.at[1, 2], mid.at[1, 2], msem.at[1, 2]).wait()
    remote(mid.at[1, 2], codes4.at[2 * up_half + core, 2], relays.at[0], crecv.at[0], down_other).start()

    pltpu.make_async_copy(send1, recv1.at[:, 1 - core], rsem1).wait()
    forward = remote(recv1.at[:, 1 - core], recv1.at[:, 1 - core], fsem1, gsem1, twin)
    forward.start()
    pltpu.make_async_copy(send1, recv1.at[:, core], gsem1).wait()
    columns = jnp.concatenate([recv1[:, :, :, f].reshape(1024, 128) for f in range(3)], axis=1)
    mixed = mm(xrows[core], columns)
    for f in range(3):
        send2[:, f] = mixed[:, 128 * f : 128 * f + 128].reshape(128, 4, 128).astype(BF)

    def start2(i, c):
        to = lax.rem(chip + 1 + i, 128)
        remote(send2.at[to], recv2.at[chip], ssem2, rsem2, (to // 2, 2 * lax.rem(to, 2) + core)).start()
        return c

    lax.fori_loop(0, 127, start2, 0)
    own2 = pltpu.make_async_copy(send2.at[chip], recv2.at[chip], lsem.at[1])
    own2.start()
    pltpu.make_async_copy(mid.at[0, 3], mid.at[0, 3], msem.at[0, 3]).wait()
    remote(mid.at[0, 3], codes4.at[2 * down_half + core, 3], relays.at[0], crecv.at[1], up).start()
    pltpu.make_async_copy(mid.at[1, 3], mid.at[1, 3], msem.at[1, 3]).wait()
    remote(mid.at[1, 3], codes4.at[2 * up_half + core, 3], relays.at[0], crecv.at[1], down_other).start()
    for s in range(2):

        def flip(i, c):
            part = xrows[s, :, pl.ds(pl.multiple_of(128 * i, 128), 128)].astype(F32)
            xcols[s, pl.ds(2 * i, 2)] = part.T.reshape(2, 2, 32, 512).astype(BF)
            return c

        lax.fori_loop(0, 8, flip, 0)

    load_d.wait()
    pltpu.make_async_copy(codes4.at[0:3, 0:3], codes4.at[0:3, 0:3], crecv.at[0]).wait()
    pltpu.make_async_copy(codes4.at[0:3, 3:4], codes4.at[0:3, 3:4], crecv.at[1]).wait()
    own_codes.wait()
    for m in range(4):
        atoms[:, 384 * m : 384 * m + 384] = mm(de[...], codes4[m].reshape(288, 384)).astype(BF)
    image = nt(atoms[...], dv[...])

    pltpu.make_async_copy(send2.at[0:127], recv2.at[0:127], rsem2).wait()
    own2.wait()
    got = recv2[...].reshape(16, 4, 2, 3, 4, 128)
    target = jnp.concatenate(
        [got[:, b, h].reshape(192, 128) for h in range(2) for b in range(4)], axis=1
    )
    misfit = (image - target.astype(F32)).astype(BF)
    for d in (2, 3, 1, 0):
        m = n ^ d
        q = mm(misfit, dv[:, pl.ds(pl.multiple_of(384 * m, 384), 384)]).astype(BF)
        qsend[m] = q
        if d == 2:
            remote(qsend.at[m, 0:160], midq.at[0, 0:160], qssem.at[0], msem.at[0, 4], up).start()
        elif d == 3:
            remote(qsend.at[m, 0:160], midq.at[1, 0:160], qssem.at[0], msem.at[1, 4], down).start()
        elif d == 1:
            remote(qsend.at[m, 0:160], qrecv.at[n, 0:160], qssem.at[0], qrsem.at[0], (w, m)).start()
    for m in range(4):
        old = codes4[m].reshape(288, 384).astype(F32)
        fresh[m] = shrink(old, tn(de[...], qsend[m]))
    own_q = pltpu.make_async_copy(qsend.at[n], qrecv.at[n], lsem.at[2])
    own_q.start()
    for m in range(4):
        atoms[:, 384 * m : 384 * m + 384] = mm(de[...], fresh[m]).astype(BF)
    for h in range(2):
        for b in (0, 2):
            block = nt(atoms[...], dv[512 * h + 128 * b : 512 * h + 128 * b + 256, :])
            for k in range(2):
                part = block[:, 128 * k : 128 * k + 128]
                send3[:, 2 * (b + k) + h] = part.reshape(16, 3, 4, 128).astype(BF)

    def start3(i, c):
        to = lax.rem(chip + 1 + i, 128)
        remote(
            send3.at[to // 8, lax.rem(to, 8)], recv3.at[core, chip], ssem3, rsem3, (to // 2, 2 * lax.rem(to, 2) + core)
        ).start()
        return c

    lax.fori_loop(0, 127, start3, 0)
    own3 = pltpu.make_async_copy(send3.at[chip // 8, lax.rem(chip, 8)], recv3.at[core, chip], lsem.at[3])
    own3.start()
    pltpu.make_async_copy(midq.at[0, 0:160], midq.at[0, 0:160], msem.at[0, 4]).wait()
    remote(midq.at[0, 0:160], qrecv.at[2 * down_half + core, 0:160], relays.at[1], qrsem.at[0], up).start()
    pltpu.make_async_copy(midq.at[1, 0:160], midq.at[1, 0:160], msem.at[1, 4]).wait()
    remote(midq.at[1, 0:160], qrecv.at[2 * up_half + core, 0:160], relays.at[1], qrsem.at[0], down_other).start()
    pltpu.make_async_copy(send2.at[0:127], recv3.at[core, 0:127], rsem3).wait()
    own3.wait()
    forward3 = remote(recv3.at[core], recv3.at[core], fsem3, gsem3, twin)
    forward3.start()
    remote(qsend.at[facing, 160:176], midq.at[0, 160:176], qssem.at[1], msem.at[0, 5], up).start()
    remote(qsend.at[cross, 160:176], midq.at[1, 160:176], qssem.at[1], msem.at[1, 5], down).start()
    remote(qsend.at[facing, 176:192], midq.at[0, 176:192], qssem.at[1], msem.at[0, 6], up).start()
    remote(qsend.at[cross, 176:192], midq.at[1, 176:192], qssem.at[1], msem.at[1, 6], down).start()
    remote(qsend.at[near, 160:192], qrecv.at[n, 160:192], qssem.at[1], qrsem.at[1], (w, near)).start()
    pltpu.make_async_copy(send2, recv3.at[1 - core], gsem3).wait()

    back = sum(
        mm(
            xcols[k, :, 1 - core].reshape(512, 512),
            jnp.concatenate([recv3[k, :, f].reshape(512, 128) for f in range(3)], axis=1),
        )
        for k in range(2)
    )
    for f in range(3):
        part = jnp.maximum(back[:, 128 * f : 128 * f + 128], 0.0)
        send4[:, :, f] = part.reshape(16, 2, 16, 128).astype(BF)

    def start4(i, c):
        a = lax.rem(w // 4 + i // 2, 16)
        b = lax.rem(w + i, 2)
        to = 4 * a + 2 * (1 - core) + b
        remote(send4.at[a, b], recv4.at[w // 4, lax.rem(w, 2)], ssem4, rsem4, (to, 2 * half + bit)).start()
        return c

    lax.fori_loop(0, 32, start4, 0)
    pltpu.make_async_copy(midq.at[0, 160:176], midq.at[0, 160:176], msem.at[0, 5]).wait()
    remote(midq.at[0, 160:176], qrecv.at[2 * down_half + core, 160:176], relays.at[1], qrsem.at[1], up).start()
    pltpu.make_async_copy(midq.at[1, 160:176], midq.at[1, 160:176], msem.at[1, 5]).wait()
    remote(midq.at[1, 160:176], qrecv.at[2 * up_half + core, 160:176], relays.at[1], qrsem.at[1], down_other).start()
    pltpu.make_async_copy(midq.at[0, 176:192], midq.at[0, 176:192], msem.at[0, 6]).wait()
    remote(midq.at[0, 176:192], qrecv.at[2 * down_half + core, 176:192], relays.at[1], qrsem.at[1], up).start()
    pltpu.make_async_copy(midq.at[1, 176:192], midq.at[1, 176:192], msem.at[1, 6]).wait()
    remote(midq.at[1, 176:192], qrecv.at[2 * up_half + core, 176:192], relays.at[1], qrsem.at[1], down_other).start()

    pltpu.make_async_copy(qsend.at[0:3, 0:160], qrecv.at[0:3, 0:160], qrsem.at[0]).wait()
    pltpu.make_async_copy(qsend.at[0:3, 160:192], qrecv.at[0:3, 160:192], qrsem.at[1]).wait()
    load_codes.wait()
    own_q.wait()
    for m in range(4):
        old = mine[4 * m : 4 * m + 4].reshape(288, 384).astype(F32)
        new[4 * m : 4 * m + 4] = shrink(old, tn(de[...], qrecv[m])).reshape(4, 72, 384)

    put_low = pltpu.make_async_copy(new.at[0:8], new_low, lsem.at[4])
    put_high = pltpu.make_async_copy(new.at[8:16], new_high, lsem.at[6])
    put_low.start()
    put_high.start()
    pltpu.make_async_copy(send4, recv4, rsem4).wait()
    put_est = pltpu.make_async_copy(recv4, est, lsem.at[5])
    put_est.start()

    pltpu.make_async_copy(send1, send1, ssem1).wait()
    pltpu.make_async_copy(send1, send1, fsem1).wait()
    pltpu.make_async_copy(send2.at[0:127], send2.at[0:127], ssem2).wait()
    pltpu.make_async_copy(send2.at[0:127], send2.at[0:127], ssem3).wait()
    pltpu.make_async_copy(send2, send2, fsem3).wait()
    pltpu.make_async_copy(send4, send4, ssem4).wait()
    pltpu.make_async_copy(codes4.at[0:3, 0:3], codes4.at[0:3, 0:3], csend.at[0]).wait()
    pltpu.make_async_copy(codes4.at[0:3, 3:4], codes4.at[0:3, 3:4], csend.at[1]).wait()
    pltpu.make_async_copy(qsend.at[0:3, 0:160], qsend.at[0:3, 0:160], qssem.at[0]).wait()
    pltpu.make_async_copy(qsend.at[0:3, 160:192], qsend.at[0:3, 160:192], qssem.at[1]).wait()
    pltpu.make_async_copy(mid, mid, relays.at[0]).wait()
    pltpu.make_async_copy(midq, midq, relays.at[1]).wait()
    put_low.wait()
    put_high.wait()
    put_est.wait()


def finish(low, high, est, codes_out, estimate, flat, out, sem):
    put_low = pltpu.make_async_copy(low, codes_out.at[0:8], sem.at[0])
    put_high = pltpu.make_async_copy(high, codes_out.at[8:16], sem.at[2])
    put_low.start()
    put_high.start()
    for b in range(2):
        for f in range(48):
            flat[:, f] = est[f // 3, b, f % 3].astype(F32)
        out[:, :, 128 * b : 128 * b + 128] = flat[...].astype(BF)
    put_est = pltpu.make_async_copy(out, estimate, sem.at[1])
    put_est.start()
    put_low.wait()
    put_high.wait()
    put_est.wait()


def shards(volume, codes_in, x_transform, y_atoms, de_atoms):
    dma = pltpu.SemaphoreType.DMA
    anyspace = pl.BlockSpec(memory_space=pl.ANY)
    low, high, est = pl.pallas_call(
        kernel,
        out_shape=(
            jax.ShapeDtypeStruct((8, 72, 384), BF),
            jax.ShapeDtypeStruct((8, 72, 384), BF),
            jax.ShapeDtypeStruct((16, 2, 3, 16, 128), BF),
        ),
        in_specs=[anyspace] * 5,
        out_specs=(anyspace, anyspace, anyspace),
        scratch_shapes=[
            pltpu.VMEM((16, 48, 256), F32),
            pltpu.VMEM((16, 72, 384), BF),
            pltpu.VMEM((16, 72, 384), BF),
            pltpu.VMEM((48, 72), BF),
            pltpu.VMEM((192, 288), BF),
            pltpu.VMEM((1024, 1024), F32),
            pltpu.VMEM((2, 512, 1024), BF),
            pltpu.VMEM((2, 16, 2, 32, 512), BF),
            pltpu.VMEM((1024, 1536), BF),
            pltpu.VMEM((4, 4, 72, 384), BF),
            pltpu.VMEM((16, 2, 3, 16, 128), BF),
            pltpu.VMEM((16, 2, 2, 3, 16, 128), BF),
            pltpu.VMEM((128, 3, 4, 128), BF),
            pltpu.VMEM((128, 3, 4, 128), BF),
            pltpu.VMEM((16, 8, 3, 4, 128), BF),
            pltpu.VMEM((2, 128, 3, 4, 128), BF),
            pltpu.VMEM((16, 2, 3, 16, 128), BF),
            pltpu.VMEM((16, 2, 3, 16, 128), BF),
            pltpu.VMEM((4, 192, 384), BF),
            pltpu.VMEM((4, 192, 384), BF),
            pltpu.VMEM((192, 1536), BF),
            pltpu.VMEM((4, 288, 384), BF),
            dma((5,)),
            *[dma] * 12,
            *[dma((2,))] * 4,
            dma((7,)),
            dma((2, 7)),
            dma((2,)),
            pltpu.VMEM((2, 4, 72, 384), BF),
            pltpu.VMEM((2, 192, 384), BF),
        ],
        compiler_params=pltpu.CompilerParams(
            collective_id=0, has_side_effects=True, vmem_limit_bytes=50331648
        ),
    )(*(pltpu.with_memory_space_constraint(a, pltpu.HBM) for a in (volume, codes_in, x_transform, y_atoms, de_atoms)))
    return pl.pallas_call(
        finish,
        out_shape=(
            jax.ShapeDtypeStruct((16, 72, 384), BF),
            jax.ShapeDtypeStruct((16, 48, 256), BF),
        ),
        in_specs=[pl.BlockSpec(memory_space=pltpu.VMEM)] * 3,
        out_specs=(anyspace, anyspace),
        scratch_shapes=[
            pltpu.VMEM((16, 48, 128), F32),
            pltpu.VMEM((16, 48, 256), BF),
            dma((3,)),
        ],
        compiler_params=pltpu.CompilerParams(vmem_limit_bytes=8 * 1024 * 1024),
    )(low, high, est)


def solution(mesh):
    return jax.shard_map(
        shards,
        mesh=mesh,
        in_specs=(P("wide", None, "narrow"), P("wide", None, "narrow"), P(), P(), P()),
        out_specs=(P("wide", None, "narrow"), P("wide", None, "narrow")),
        check_vma=False,
    )
```

```python
import jax
import jax.numpy as jnp
from jax import lax
from jax.experimental import pallas as pl
from jax.experimental.pallas import tpu as pltpu
from jax.sharding import PartitionSpec as P

step_size = 0.06
threshold = 0.05
BF = jnp.bfloat16
F32 = jnp.float32
MESH = pl.DeviceIdType.MESH


def mm(a, b):
    return jnp.dot(a, b, preferred_element_type=F32)


def nt(a, b):
    return lax.dot_general(a, b, (((1,), (1,)), ((), ())), preferred_element_type=F32)


def tn(a, b):
    return lax.dot_general(a, b, (((0,), (0,)), ((), ())), preferred_element_type=F32)


def shrink(codes, grads):
    moved = codes - step_size * grads
    return (moved - jnp.clip(moved, -threshold, threshold)).astype(BF)


def remote(src, dst, send, recv, device):
    return pltpu.make_async_remote_copy(
        src_ref=src, dst_ref=dst, send_sem=send, recv_sem=recv, device_id=device, device_id_type=MESH
    )


def kernel(
    vol_in, codes, xin, din, de_in,
    new_low, new_high, est,
    vol, mine, new, de_small, de, xv, xrows, xcols, dv, codes4, send1, recv1, send2, recv2, send3, recv3, send4, recv4, qsend, qrecv, atoms, fresh,
    load, ssem1, rsem1, fsem1, gsem1, ssem2, rsem2, ssem3, rsem3, fsem3, gsem3, ssem4, rsem4,
    csend, crecv, qssem, qrsem, lsem, msem, relays, mid, midq,
):
    w = lax.axis_index("wide")
    n = lax.axis_index("narrow")
    half = n // 2
    core = n % 2
    chip = 2 * w + half
    twin = (w, 2 * half + 1 - core)
    bit = lax.rem(w // 2, 2)
    low = lax.rem(w, 4)
    across = w - low + lax.rem(low + 2, 4)
    up_half = lax.rem(half + low // 2, 2)
    down_half = 1 - up_half
    up = (across, 2 * up_half + core)
    down = (across, 2 * down_half + core)
    down_other = (across, 2 * down_half + 1 - core)
    near = n + 1 - 2 * core
    facing = lax.rem(n + 2, 4)
    cross = 2 * (1 - half) + 1 - core

    loads = [
        pltpu.make_async_copy(src, dst, load.at[i])
        for i, (src, dst) in enumerate(((vol_in, vol), (xin, xv), (de_in, de_small), (din, dv), (codes, mine)))
    ]
    load_vol, load_x, load_de, load_d, load_codes = loads
    load_vol.start()

    barrier = pltpu.get_barrier_semaphore()

    def greet_from(i, c):
        frm = 4 * (i // 2) + 2 * (1 - core) + lax.rem(i, 2)
        pl.semaphore_signal(barrier, inc=1, device_id=(frm, 2 * half + bit), device_id_type=MESH)
        return c

    for d in (1, 2, 3):
        pl.semaphore_signal(barrier, inc=1, device_id=(w, lax.rem(n + d, 4)), device_id_type=MESH)
    for to in (up, down, (across, 2 * up_half + 1 - core)):
        pl.semaphore_signal(barrier, inc=1, device_id=to, device_id_type=MESH)
    lax.fori_loop(0, 32, greet_from, 0)

    for copy in loads[1:]:
        copy.start()
    load_vol.wait()
    for f in range(48):
        rows = vol[:, f, :].astype(BF)
        for b in range(2):
            send1[f // 3, b, f % 3] = rows[:, 128 * b : 128 * b + 128]

    pl.semaphore_wait(barrier, 38)

    def start1(i, c):
        t = lax.rem(w // 4 + i // 2, 16)
        b = lax.rem(w + i, 2)
        remote(
            send1.at[t, b], recv1.at[w // 4, bit, lax.rem(w, 2)], ssem1, rsem1, (4 * t + 2 * core + b, 2 * half + 1 - bit)
        ).start()
        return c

    lax.fori_loop(0, 32, start1, 0)
    remote(codes.at[4 * facing + 0], mid.at[0, 0], csend.at[0], msem.at[0, 0], up).start()
    remote(codes.at[4 * cross + 0], mid.at[1, 0], csend.at[0], msem.at[1, 0], down).start()
    remote(codes.at[4 * facing + 1], mid.at[0, 1], csend.at[0], msem.at[0, 1], up).start()
    remote(codes.at[4 * cross + 1], mid.at[1, 1], csend.at[0], msem.at[1, 1], down).start()
    remote(codes.at[4 * facing + 2], mid.at[0, 2], csend.at[0], msem.at[0, 2], up).start()
    remote(codes.at[4 * cross + 2], mid.at[1, 2], csend.at[0], msem.at[1, 2], down).start()
    remote(codes.at[pl.ds(4 * near + 0, 3)], codes4.at[n, 0:3], csend.at[0], crecv.at[0], (w, near)).start()
    remote(codes.at[4 * facing + 3], mid.at[0, 3], csend.at[1], msem.at[0, 3], up).start()
    remote(codes.at[4 * cross + 3], mid.at[1, 3], csend.at[1], msem.at[1, 3], down).start()
    remote(codes.at[pl.ds(4 * near + 3, 1)], codes4.at[n, 3:4], csend.at[1], crecv.at[1], (w, near)).start()
    own_codes = pltpu.make_async_copy(codes.at[pl.ds(4 * n, 4)], codes4.at[n], lsem.at[0])
    own_codes.start()

    load_x.wait()

    def group_rows(i, c):
        rows = xv[pl.ds(pl.multiple_of(64 * i, 64), 64), :].reshape(8, 8, 1024)
        for s in range(2):
            xrows[s, pl.ds(pl.multiple_of(32 * i, 32), 32), :] = rows[:, 4 * s : 4 * s + 4].reshape(32, 1024).astype(BF)
        return c

    lax.fori_loop(0, 16, group_rows, 0)

    load_de.wait()
    spread = (lax.broadcasted_iota(jnp.int32, (192, 48), 0) // 4 == lax.broadcasted_iota(jnp.int32, (192, 48), 1))
    tile = (lax.rem(lax.broadcasted_iota(jnp.int32, (72, 288), 1), 72) == lax.broadcasted_iota(jnp.int32, (72, 288), 0))
    tall = mm(spread.astype(F32).astype(BF), de_small[...]).astype(BF)
    wide = mm(tall, tile.astype(F32).astype(BF))
    same = lax.rem(lax.broadcasted_iota(jnp.int32, (192, 288), 0), 4) == lax.broadcasted_iota(jnp.int32, (192, 288), 1) // 72
    de[...] = jnp.where(same, wide, 0.0).astype(BF)

    pltpu.make_async_copy(mid.at[0, 0], mid.at[0, 0], msem.at[0, 0]).wait()
    remote(mid.at[0, 0], codes4.at[2 * down_half + core, 0], relays.at[0], crecv.at[0], up).start()
    pltpu.make_async_copy(mid.at[1, 0], mid.at[1, 0], msem.at[1, 0]).wait()
    remote(mid.at[1, 0], codes4.at[2 * up_half + core, 0], relays.at[0], crecv.at[0], down_other).start()
    pltpu.make_async_copy(mid.at[0, 1], mid.at[0, 1], msem.at[0, 1]).wait()
    remote(mid.at[0, 1], codes4.at[2 * down_half + core, 1], relays.at[0], crecv.at[0], up).start()
    pltpu.make_async_copy(mid.at[1, 1], mid.at[1, 1], msem.at[1, 1]).wait()
    remote(mid.at[1, 1], codes4.at[2 * up_half + core, 1], relays.at[0], crecv.at[0], down_other).start()
    pltpu.make_async_copy(mid.at[0, 2], mid.at[0, 2], msem.at[0, 2]).wait()
    remote(mid.at[0, 2], codes4.at[2 * down_half + core, 2], relays.at[0], crecv.at[0], up).start()
    pltpu.make_async_copy(mid.at[1, 2], mid.at[1, 2], msem.at[1, 2]).wait()
    remote(mid.at[1, 2], codes4.at[2 * up_half + core, 2], relays.at[0], crecv.at[0], down_other).start()

    pltpu.make_async_copy(send1, recv1.at[:, 1 - core], rsem1).wait()
    forward = remote(recv1.at[:, 1 - core], recv1.at[:, 1 - core], fsem1, gsem1, twin)
    forward.start()
    pltpu.make_async_copy(send1, recv1.at[:, core], gsem1).wait()
    columns = jnp.concatenate([recv1[:, :, :, f].reshape(1024, 128) for f in range(3)], axis=1)
    mixed = mm(xrows[core], columns)
    for f in range(3):
        send2[:, f] = mixed[:, 128 * f : 128 * f + 128].reshape(128, 4, 128).astype(BF)

    def start2(i, c):
        to = lax.rem(chip + 1 + i, 128)
        remote(send2.at[to], recv2.at[chip], ssem2, rsem2, (to // 2, 2 * lax.rem(to, 2) + core)).start()
        return c

    lax.fori_loop(0, 127, start2, 0)
    own2 = pltpu.make_async_copy(send2.at[chip], recv2.at[chip], lsem.at[1])
    own2.start()
    pltpu.make_async_copy(mid.at[0, 3], mid.at[0, 3], msem.at[0, 3]).wait()
    remote(mid.at[0, 3], codes4.at[2 * down_half + core, 3], relays.at[0], crecv.at[1], up).start()
    pltpu.make_async_copy(mid.at[1, 3], mid.at[1, 3], msem.at[1, 3]).wait()
    remote(mid.at[1, 3], codes4.at[2 * up_half + core, 3], relays.at[0], crecv.at[1], down_other).start()
    for s in range(2):

        def flip(i, c):
            part = xrows[s, :, pl.ds(pl.multiple_of(128 * i, 128), 128)].astype(F32)
            xcols[s, pl.ds(2 * i, 2)] = part.T.reshape(2, 2, 32, 512).astype(BF)
            return c

        lax.fori_loop(0, 8, flip, 0)

    load_d.wait()
    pltpu.make_async_copy(codes4.at[0:3, 0:3], codes4.at[0:3, 0:3], crecv.at[0]).wait()
    pltpu.make_async_copy(codes4.at[0:3, 3:4], codes4.at[0:3, 3:4], crecv.at[1]).wait()
    own_codes.wait()
    for m in range(4):
        atoms[:, 384 * m : 384 * m + 384] = mm(de[...], codes4[m].reshape(288, 384)).astype(BF)
    image = nt(atoms[...], dv[...])

    pltpu.make_async_copy(send2.at[0:127], recv2.at[0:127], rsem2).wait()
    own2.wait()
    got = recv2[...].reshape(16, 4, 2, 3, 4, 128)
    target = jnp.concatenate(
        [got[:, b, h].reshape(192, 128) for h in range(2) for b in range(4)], axis=1
    )
    misfit = (image - target.astype(F32)).astype(BF)
    for d in (2, 3, 1, 0):
        m = n ^ d
        q = mm(misfit, dv[:, pl.ds(pl.multiple_of(384 * m, 384), 384)]).astype(BF)
        qsend[m] = q
        if d == 2:
            remote(qsend.at[m, 0:160], midq.at[0, 0:160], qssem.at[0], msem.at[0, 4], up).start()
        elif d == 3:
            remote(qsend.at[m, 0:160], midq.at[1, 0:160], qssem.at[0], msem.at[1, 4], down).start()
        elif d == 1:
            remote(qsend.at[m, 0:160], qrecv.at[n, 0:160], qssem.at[0], qrsem.at[0], (w, m)).start()
    for m in range(4):
        old = codes4[m].reshape(288, 384).astype(F32)
        fresh[m] = shrink(old, tn(de[...], qsend[m]))
    own_q = pltpu.make_async_copy(qsend.at[n], qrecv.at[n], lsem.at[2])
    own_q.start()
    for m in range(4):
        atoms[:, 384 * m : 384 * m + 384] = mm(de[...], fresh[m]).astype(BF)
    plane = 4 * half + low
    for turn in range(4):
        pair = lax.rem(plane // 2 + 1 + turn, 4)
        block = nt(atoms[...], dv[pl.ds(pl.multiple_of(256 * pair, 256), 256), :])
        for k in range(2):
            part = block[:, 128 * k : 128 * k + 128]
            send3[:, 4 * lax.rem(pair, 2) + 2 * k + pair // 2] = part.reshape(16, 3, 4, 128).astype(BF)

        def start3(i, c):
            t = lax.rem(w // 4 + 1 + i // 2, 16)
            k = lax.rem(plane + 1 + i, 2)
            b = 2 * lax.rem(pair, 2) + k
            h = pair // 2
            remote(
                send3.at[t, 2 * b + h], recv3.at[core, chip], ssem3, rsem3, (4 * t + b, 2 * h + core)
            ).start()
            return c

        lax.fori_loop(0, 32 if turn < 3 else 31, start3, 0)

    own3 = pltpu.make_async_copy(send3.at[chip // 8, lax.rem(chip, 8)], recv3.at[core, chip], lsem.at[3])
    own3.start()
    pltpu.make_async_copy(midq.at[0, 0:160], midq.at[0, 0:160], msem.at[0, 4]).wait()
    remote(midq.at[0, 0:160], qrecv.at[2 * down_half + core, 0:160], relays.at[1], qrsem.at[0], up).start()
    pltpu.make_async_copy(midq.at[1, 0:160], midq.at[1, 0:160], msem.at[1, 4]).wait()
    remote(midq.at[1, 0:160], qrecv.at[2 * up_half + core, 0:160], relays.at[1], qrsem.at[0], down_other).start()
    pltpu.make_async_copy(send2.at[0:127], recv3.at[core, 0:127], rsem3).wait()
    own3.wait()
    forward3 = remote(recv3.at[core], recv3.at[core], fsem3, gsem3, twin)
    forward3.start()
    remote(qsend.at[facing, 160:176], midq.at[0, 160:176], qssem.at[1], msem.at[0, 5], up).start()
    remote(qsend.at[cross, 160:176], midq.at[1, 160:176], qssem.at[1], msem.at[1, 5], down).start()
    remote(qsend.at[facing, 176:192], midq.at[0, 176:192], qssem.at[1], msem.at[0, 6], up).start()
    remote(qsend.at[cross, 176:192], midq.at[1, 176:192], qssem.at[1], msem.at[1, 6], down).start()
    remote(qsend.at[near, 160:192], qrecv.at[n, 160:192], qssem.at[1], qrsem.at[1], (w, near)).start()
    pltpu.make_async_copy(send2, recv3.at[1 - core], gsem3).wait()

    back = sum(
        mm(
            xcols[k, :, 1 - core].reshape(512, 512),
            jnp.concatenate([recv3[k, :, f].reshape(512, 128) for f in range(3)], axis=1),
        )
        for k in range(2)
    )
    for f in range(3):
        part = jnp.maximum(back[:, 128 * f : 128 * f + 128], 0.0)
        send4[:, :, f] = part.reshape(16, 2, 16, 128).astype(BF)

    def start4(i, c):
        a = lax.rem(w // 4 + i // 2, 16)
        b = lax.rem(w + i, 2)
        to = 4 * a + 2 * (1 - core) + b
        remote(send4.at[a, b], recv4.at[w // 4, lax.rem(w, 2)], ssem4, rsem4, (to, 2 * half + bit)).start()
        return c

    lax.fori_loop(0, 32, start4, 0)
    pltpu.make_async_copy(midq.at[0, 160:176], midq.at[0, 160:176], msem.at[0, 5]).wait()
    remote(midq.at[0, 160:176], qrecv.at[2 * down_half + core, 160:176], relays.at[1], qrsem.at[1], up).start()
    pltpu.make_async_copy(midq.at[1, 160:176], midq.at[1, 160:176], msem.at[1, 5]).wait()
    remote(midq.at[1, 160:176], qrecv.at[2 * up_half + core, 160:176], relays.at[1], qrsem.at[1], down_other).start()
    pltpu.make_async_copy(midq.at[0, 176:192], midq.at[0, 176:192], msem.at[0, 6]).wait()
    remote(midq.at[0, 176:192], qrecv.at[2 * down_half + core, 176:192], relays.at[1], qrsem.at[1], up).start()
    pltpu.make_async_copy(midq.at[1, 176:192], midq.at[1, 176:192], msem.at[1, 6]).wait()
    remote(midq.at[1, 176:192], qrecv.at[2 * up_half + core, 176:192], relays.at[1], qrsem.at[1], down_other).start()

    pltpu.make_async_copy(qsend.at[0:3, 0:160], qrecv.at[0:3, 0:160], qrsem.at[0]).wait()
    pltpu.make_async_copy(qsend.at[0:3, 160:192], qrecv.at[0:3, 160:192], qrsem.at[1]).wait()
    load_codes.wait()
    own_q.wait()
    for m in range(4):
        old = mine[4 * m : 4 * m + 4].reshape(288, 384).astype(F32)
        new[4 * m : 4 * m + 4] = shrink(old, tn(de[...], qrecv[m])).reshape(4, 72, 384)

    put_low = pltpu.make_async_copy(new.at[0:8], new_low, lsem.at[4])
    put_high = pltpu.make_async_copy(new.at[8:16], new_high, lsem.at[6])
    put_low.start()
    put_high.start()
    pltpu.make_async_copy(send4, recv4, rsem4).wait()
    put_est = pltpu.make_async_copy(recv4, est, lsem.at[5])
    put_est.start()

    pltpu.make_async_copy(send1, send1, ssem1).wait()
    pltpu.make_async_copy(send1, send1, fsem1).wait()
    pltpu.make_async_copy(send2.at[0:127], send2.at[0:127], ssem2).wait()
    pltpu.make_async_copy(send2.at[0:127], send2.at[0:127], ssem3).wait()
    pltpu.make_async_copy(send2, send2, fsem3).wait()
    pltpu.make_async_copy(send4, send4, ssem4).wait()
    pltpu.make_async_copy(codes4.at[0:3, 0:3], codes4.at[0:3, 0:3], csend.at[0]).wait()
    pltpu.make_async_copy(codes4.at[0:3, 3:4], codes4.at[0:3, 3:4], csend.at[1]).wait()
    pltpu.make_async_copy(qsend.at[0:3, 0:160], qsend.at[0:3, 0:160], qssem.at[0]).wait()
    pltpu.make_async_copy(qsend.at[0:3, 160:192], qsend.at[0:3, 160:192], qssem.at[1]).wait()
    pltpu.make_async_copy(mid, mid, relays.at[0]).wait()
    pltpu.make_async_copy(midq, midq, relays.at[1]).wait()
    put_low.wait()
    put_high.wait()
    put_est.wait()


def finish(low, high, est, codes_out, estimate, flat, out, sem):
    put_low = pltpu.make_async_copy(low, codes_out.at[0:8], sem.at[0])
    put_high = pltpu.make_async_copy(high, codes_out.at[8:16], sem.at[2])
    put_low.start()
    put_high.start()
    for b in range(2):
        for f in range(48):
            flat[:, f] = est[f // 3, b, f % 3].astype(F32)
        out[:, :, 128 * b : 128 * b + 128] = flat[...].astype(BF)
    put_est = pltpu.make_async_copy(out, estimate, sem.at[1])
    put_est.start()
    put_low.wait()
    put_high.wait()
    put_est.wait()


def shards(volume, codes_in, x_transform, y_atoms, de_atoms):
    dma = pltpu.SemaphoreType.DMA
    anyspace = pl.BlockSpec(memory_space=pl.ANY)
    low, high, est = pl.pallas_call(
        kernel,
        out_shape=(
            jax.ShapeDtypeStruct((8, 72, 384), BF),
            jax.ShapeDtypeStruct((8, 72, 384), BF),
            jax.ShapeDtypeStruct((16, 2, 3, 16, 128), BF),
        ),
        in_specs=[anyspace] * 5,
        out_specs=(anyspace, anyspace, anyspace),
        scratch_shapes=[
            pltpu.VMEM((16, 48, 256), F32),
            pltpu.VMEM((16, 72, 384), BF),
            pltpu.VMEM((16, 72, 384), BF),
            pltpu.VMEM((48, 72), BF),
            pltpu.VMEM((192, 288), BF),
            pltpu.VMEM((1024, 1024), F32),
            pltpu.VMEM((2, 512, 1024), BF),
            pltpu.VMEM((2, 16, 2, 32, 512), BF),
            pltpu.VMEM((1024, 1536), BF),
            pltpu.VMEM((4, 4, 72, 384), BF),
            pltpu.VMEM((16, 2, 3, 16, 128), BF),
            pltpu.VMEM((16, 2, 2, 3, 16, 128), BF),
            pltpu.VMEM((128, 3, 4, 128), BF),
            pltpu.VMEM((128, 3, 4, 128), BF),
            pltpu.VMEM((16, 8, 3, 4, 128), BF),
            pltpu.VMEM((2, 128, 3, 4, 128), BF),
            pltpu.VMEM((16, 2, 3, 16, 128), BF),
            pltpu.VMEM((16, 2, 3, 16, 128), BF),
            pltpu.VMEM((4, 192, 384), BF),
            pltpu.VMEM((4, 192, 384), BF),
            pltpu.VMEM((192, 1536), BF),
            pltpu.VMEM((4, 288, 384), BF),
            dma((5,)),
            *[dma] * 12,
            *[dma((2,))] * 4,
            dma((7,)),
            dma((2, 7)),
            dma((2,)),
            pltpu.VMEM((2, 4, 72, 384), BF),
            pltpu.VMEM((2, 192, 384), BF),
        ],
        compiler_params=pltpu.CompilerParams(
            collective_id=0, has_side_effects=True, vmem_limit_bytes=50331648
        ),
    )(*(pltpu.with_memory_space_constraint(a, pltpu.HBM) for a in (volume, codes_in, x_transform, y_atoms, de_atoms)))
    return pl.pallas_call(
        finish,
        out_shape=(
            jax.ShapeDtypeStruct((16, 72, 384), BF),
            jax.ShapeDtypeStruct((16, 48, 256), BF),
        ),
        in_specs=[pl.BlockSpec(memory_space=pltpu.VMEM)] * 3,
        out_specs=(anyspace, anyspace),
        scratch_shapes=[
            pltpu.VMEM((16, 48, 128), F32),
            pltpu.VMEM((16, 48, 256), BF),
            dma((3,)),
        ],
        compiler_params=pltpu.CompilerParams(vmem_limit_bytes=8 * 1024 * 1024),
    )(low, high, est)


def solution(mesh):
    return jax.shard_map(
        shards,
        mesh=mesh,
        in_specs=(P("wide", None, "narrow"), P("wide", None, "narrow"), P(), P(), P()),
        out_specs=(P("wide", None, "narrow"), P("wide", None, "narrow")),
        check_vma=False,
    )
```
